256 devices in a mesh: outer: 8 (over z), inner: 32 (over x, y, core).
Axes of the slice: x: 4, y: 4, z: 8, core: 2. Of those that a mesh axis runs over, the one named last changes fastest.
Arguments:
- observed: float32 [262144, 768], P(('outer', 'inner')), may hold values from -6 to 6
- leaf_order: int32 [256, 1024], P(('outer', 'inner')), may hold values from 0 to 1023, each once within a row
- leaf_inverse: bfloat16 [262144, 1024], P(('outer', 'inner')), may hold values from -0.1875 to 0.1875
- project_basis: bfloat16 [262144, 1024], P(('outer', 'inner')), may hold values from -0.1875 to 0.1875
- correct_basis: bfloat16 [262144, 1024], P(('outer', 'inner')), may hold values from -0.375 to 0.375
- coupling: bfloat16 [65536, 256], P(('outer', 'inner'))
- trend_basis: bfloat16 [262144, 256], P(('outer', 'inner')), may hold values from -0.1875 to 0.1875
- trend_correct: bfloat16 [262144, 256], P(('outer', 'inner')), may hold values from -0.375 to 0.375
Outputs:
- solution: float32 [262144, 768], P(('outer', 'inner'))
The draws below stay inside these ranges and needn't reach their ends.
All inputs are finite; a program needn't handle non-finite values.
Results may differ from the reference program's by a relative error of at most 0.013.
Values may be sent and summed in bfloat16 or wider, within the bound.
No kernel may reach another device: no remote copies, remote signals or barrier semaphores. Data moves between devices by JAX's collectives and lax.ppermute only.
A program may use at most 64 MiB of HBM per device.

```python
import math
import jax
import jax.numpy as jnp
from jax import lax

LEAF = 1024
RANK = 128
COLS = 768
LEVELS = 8
NPTS = 262144
DEVICES = 256


def draw_coupling(key, part):
    total_rows = DEVICES * 2 * RANK
    row_ids = jnp.arange(total_rows, dtype=jnp.int32)
    slot_ids = row_ids // (2 * RANK)
    lowest = jnp.where(slot_ids == 0, DEVICES, jnp.bitwise_and(slot_ids, -slot_ids))
    scales = 1.0 / jnp.sqrt(lowest.astype(jnp.float32))
    noise = jax.random.normal(key, (total_rows, 2 * RANK), jnp.float32)
    within = row_ids % (2 * RANK)
    column_ids = jnp.arange(2 * RANK, dtype=jnp.int32)
    identity = (within[:, None] == column_ids[None, :]).astype(jnp.float32)
    matrix = (0.5 * identity + 0.5 / math.sqrt(2 * RANK) * noise) * scales[:, None]
    return matrix.astype(jnp.bfloat16)


def block_levels(own_key, shape, split, low, largest):
    factor_of, own = 1.0, jax.random.fold_in(own_key, 6)
    for dim, blocks in split:
        heights = jnp.exp(jax.random.uniform(jax.random.fold_in(own, dim), (blocks,), jnp.float32, low / len(split), largest / len(split)))
        factor_of = factor_of * jnp.repeat(heights, shape[dim] // blocks).reshape([-1 if axis == dim else 1 for axis in range(len(shape))])
    return factor_of


def centred(key, dims, deviation, bound, split=(), kind=jnp.bfloat16):
    level = block_levels(key, dims, split, -0.22, 0.18) if split else 1.0
    drawn = jax.random.normal(key, dims, jnp.float32) * deviation * level
    return jnp.minimum(jnp.maximum(drawn, -bound), bound).astype(kind)


def setup_inputs(seed: int = 0) -> dict:
    key_of = jax.random.split(jax.random.key(seed), 9)
    observed = centred(key_of[0], (NPTS, COLS), 1.0, 6.0, ((0, 256),), jnp.float32)
    leaf_order = jax.vmap(lambda own: jax.random.permutation(own, LEAF))(jax.random.split(key_of[1], DEVICES)).reshape((DEVICES, LEAF)).astype(jnp.int32)
    leaf_inverse = centred(key_of[2], (NPTS, LEAF), LEAF ** -0.5, 0.1875, ((0, 256),))
    project_basis = centred(key_of[3], (NPTS, LEVELS * RANK), LEAF ** -0.5, 0.1875, ((0, 256),))
    correct_basis = centred(key_of[4], (NPTS, LEVELS * RANK), (2 * RANK) ** -0.5, 0.375, ((0, 256),))
    coupling = draw_coupling(jax.random.fold_in(key_of[8], 71), 0)
    trend_basis = centred(key_of[6], (NPTS, 2 * RANK), LEAF ** -0.5, 0.1875, ((0, 256),))
    trend_correct = centred(key_of[7], (NPTS, 2 * RANK), (2 * RANK) ** -0.5, 0.375, ((0, 256),))
    return dict(observed=observed, leaf_order=leaf_order, leaf_inverse=leaf_inverse, project_basis=project_basis, correct_basis=correct_basis, coupling=coupling, trend_basis=trend_basis, trend_correct=trend_correct)


def rounded(values):
    return lax.optimization_barrier(values.astype(jnp.bfloat16)).astype(jnp.float32)


def reference(observed, leaf_order, leaf_inverse, project_basis, correct_basis, coupling, trend_basis, trend_correct):
    leaves = DEVICES
    blocks = observed.reshape(leaves, LEAF, COLS)
    ordered = jax.vmap(lambda block, index: block[index])(blocks, leaf_order)
    inverse = leaf_inverse.reshape(leaves, LEAF, LEAF).astype(jnp.float32)
    estimate = jnp.einsum("nij,njc->nic", inverse, rounded(ordered))
    project_all = project_basis.reshape(leaves, LEAF, LEVELS * RANK)
    correct_all = correct_basis.reshape(leaves, LEAF, LEVELS * RANK)
    blocks_all = coupling.reshape(leaves, 2 * RANK, 2 * RANK)
    for level_no in range(1, LEVELS + 1):
        child = 2 ** (level_no - 1)
        nodes = leaves // (2 * child)
        estimate_bf = rounded(estimate)
        basis = project_all[:, :, (level_no - 1) * RANK:level_no * RANK].astype(jnp.float32)
        projection = jnp.einsum("nkr,nkc->nrc", basis, estimate_bf)
        child_sum = projection.reshape(nodes * 2, child, RANK, COLS).sum(axis=1)
        stacked = child_sum.reshape(nodes, 2 * RANK, COLS)
        owners = (jnp.arange(nodes, dtype=jnp.int32) * (2 * child) + child).astype(jnp.int32)
        matrices = blocks_all[owners].astype(jnp.float32)
        factor = rounded(jnp.einsum("nij,njc->nic", matrices, stacked, precision=lax.Precision.HIGHEST))
        halves = jnp.repeat(factor.reshape(nodes * 2, RANK, COLS), child, axis=0)
        columns = correct_all[:, :, (level_no - 1) * RANK:level_no * RANK].astype(jnp.float32)
        estimate = estimate - jnp.einsum("nkr,nrc->nkc", columns, halves)
    trend_in = trend_basis.reshape(leaves, LEAF, 2 * RANK).astype(jnp.float32)
    trend_sum = jnp.einsum("nkr,nkc->rc", trend_in, rounded(estimate))
    trend_factor = rounded(jnp.dot(blocks_all[0].astype(jnp.float32), rounded(trend_sum)))
    trend_out = trend_correct.reshape(leaves, LEAF, 2 * RANK).astype(jnp.float32)
    solution = estimate - jnp.einsum("nkr,rc->nkc", trend_out, trend_factor)
    return solution.reshape(NPTS, COLS)
```

```python
import jax
import jax.numpy as jnp
from jax import lax
from jax.experimental import pallas as pl
from jax.experimental.pallas import tpu as pltpu
from jax.sharding import PartitionSpec as P


BF = jnp.bfloat16
F32 = jnp.float32
RK = 128
NC = 96
HALF = 384


def nn(a, b):
    return lax.dot_general(a, b, (((1,), (0,)), ((), ())), preferred_element_type=F32)


def nt(a, b):
    return lax.dot_general(a, b, (((1,), (1,)), ((), ())), preferred_element_type=F32)


def tn(a, b):
    return lax.dot_general(a, b, (((0,), (0,)), ((), ())), preferred_element_type=F32)


def core_of():
    return lax.axis_index("inner") & 1


def ypos_of():
    return (lax.axis_index("inner") >> 1) & 3


def side_of(bit):
    if bit < 5:
        return (lax.axis_index("inner") >> bit) & 1
    return (lax.axis_index("outer") >> (bit - 5)) & 1


def flip(value, bit):
    axis, mask = ("inner", 1 << bit) if bit < 5 else ("outer", 1 << (bit - 5))
    size = 32 if bit < 5 else 8
    return lax.ppermute(value, axis, [(i, i ^ mask) for i in range(size)])


def turn(value, shift):
    pairs = []
    for i in range(32):
        x, y, c = i >> 3, (i >> 1) & 3, i & 1
        pairs.append((i, x * 8 + ((y + shift) & 3) * 2 + c))
    return lax.ppermute(value, "inner", pairs)


def kcall(fn, name, outs, args, scratch=(), flops=0):
    size = sum(a.size * a.dtype.itemsize for a in args)
    size += sum(o.size * o.dtype.itemsize for o in outs)
    return pl.pallas_call(
        fn,
        out_shape=tuple(outs),
        scratch_shapes=list(scratch),
        name=name,
        cost_estimate=pl.CostEstimate(flops=flops, bytes_accessed=size, transcendentals=0),
    )(*args)


def sds(shape, dtype=BF):
    return jax.ShapeDtypeStruct(shape, dtype)


def leaf_kernel(order_ref, obs_ref, inv_ref, basis_ref, est_ref, estt_ref, proj_ref, pick):
    @pl.when(pl.program_id(0) == 0)
    def _():
        for b in range(8):
            row = order_ref[:, b * 128 : (b + 1) * 128].astype(F32)
            col = jnp.transpose(jnp.broadcast_to(row, (128, 128)))
            for q in range(8):
                lane = lax.broadcasted_iota(jnp.int32, (128, 128), 1) + q * 128
                hit = col == lane.astype(F32)
                pick[b * 128 : (b + 1) * 128, q * 128 : (q + 1) * 128] = jnp.where(
                    hit, 1.0, 0.0
                ).astype(BF)

    ordered = nn(pick[...], obs_ref[...].astype(BF)).astype(BF)
    est = nn(inv_ref[...], ordered)
    est_ref[...] = est
    estt = jnp.transpose(est.astype(BF))
    estt_ref[...] = estt
    proj_ref[...] = nn(estt, basis_ref[...]).astype(BF)


def leaf_product(order, observed, inverse, basis):
    cols = 256
    return pl.pallas_call(
        leaf_kernel,
        grid=(768 // cols,),
        in_specs=[
            pl.BlockSpec((1, 1024), lambda j: (0, 0)),
            pl.BlockSpec((1024, cols), lambda j: (0, j)),
            pl.BlockSpec((1024, 1024), lambda j: (0, 0)),
            pl.BlockSpec((1024, RK), lambda j: (0, 0)),
        ],
        out_specs=[
            pl.BlockSpec((1024, cols), lambda j: (0, j)),
            pl.BlockSpec((cols, 1024), lambda j: (j, 0)),
            pl.BlockSpec((cols, RK), lambda j: (j, 0)),
        ],
        out_shape=[sds((1024, 768), F32), sds((768, 1024)), sds((768, RK))],
        scratch_shapes=[pltpu.VMEM((1024, 1024), BF)],
        name="leaf",
        cost_estimate=pl.CostEstimate(flops=3500000000, bytes_accessed=12000000, transcendentals=0),
    )(order, observed, inverse, basis)


def project_kernel(estt_ref, u_ref, t_ref, out_ref):
    estt = estt_ref[...]
    out_ref[:, :896] = nn(estt, u_ref[:, 128:]).astype(BF)
    out_ref[:, 896:] = nn(estt, t_ref[...]).astype(BF)


def project(estt, basis, trend):
    return pl.pallas_call(
        project_kernel,
        grid=(3,),
        in_specs=[
            pl.BlockSpec((256, 1024), lambda j: (j, 0)),
            pl.BlockSpec((1024, 1024), lambda j: (0, 0)),
            pl.BlockSpec((1024, 256), lambda j: (0, 0)),
        ],
        out_specs=pl.BlockSpec((256, 1152), lambda j: (j, 0)),
        out_shape=sds((768, 1152)),
        name="project",
        cost_estimate=pl.CostEstimate(flops=1800000000, bytes_accessed=6000000, transcendentals=0),
    )(estt, basis, trend)


GOFF = {}
_at = 0
for _k in range(2, 9):
    GOFF[_k] = _at
    _at += (10 - _k) * 128
GW = _at


def gram_kernel(u_ref, v_ref, t_ref, first_ref, send_ref, keep_ref, whole):
    c = core_of()
    for k in range(1, 9):
        v = v_ref[:, (k - 1) * 128 : k * 128]
        vt = jnp.transpose(v)
        wide = (8 - k) * 128
        at = 0 if k == 1 else GOFF[k]
        if wide:
            left = nn(vt, u_ref[:, k * 128 :])
            if k == 1:
                first_ref[:, :wide] = left.astype(BF)
            else:
                whole[:, at : at + wide] = left
        right = nn(vt, t_ref[...])
        if k == 1:
            first_ref[:, wide:] = right.astype(BF)
        else:
            whole[:, at + wide : at + wide + 256] = right
    send_ref[...] = whole[pl.ds(pl.multiple_of((1 - c) * 64, 64), 64), :].astype(BF)
    keep_ref[...] = whole[pl.ds(pl.multiple_of(c * 64, 64), 64), :].astype(BF)


AW = 1920 + 512
BW = GW - 1920


def chip_gram_kernel(keep_ref, recv_ref, kown_ref, krecv_ref, a_ref, b0, b1, b2, b3, whole, kboth):
    c = core_of()
    y = ypos_of()
    total = keep_ref[...].astype(F32) + recv_ref[...].astype(F32)
    a_ref[:, :1920] = total[:, :1920].astype(BF)
    kboth[c] = kown_ref[...]
    kboth[1 - c] = krecv_ref[...]
    for i in range(2):
        a_ref[:, 1920 + i * 256 : 2176 + i * 256] = kboth[
            0, pl.ds(pl.multiple_of(c * 128 + i * 64, 64), 64), :
        ]
    whole[...] = total[:, 1920:]
    for s, out in enumerate((b0, b1, b2, b3)):
        start = pl.multiple_of(((y + s) & 3) * 16, 16)
        out[...] = whole[pl.ds(start, 16), :].astype(BF)


def group_gram_kernel(b0, b1, b2, b3, a0, a1, a2, a3, out_ref):
    y = ypos_of()
    total = b0[...].astype(F32) + b1[...].astype(F32) + b2[...].astype(F32) + b3[...].astype(F32)
    out_ref[:, :BW] = total.astype(BF)
    for s, a in enumerate((a0, a1, a2, a3)):

        @pl.when(y == s)
        def _(a=a, s=s):
            out_ref[:, BW:] = a[s * 16 : s * 16 + 16, 1920:]


def step_gram_kernel(bit, wide, own_ref, recv_ref, pair_ref, next_ref, both):
    side = side_of(bit)
    both[side] = own_ref[...]
    both[1 - side] = recv_ref[...]
    rest = own_ref.shape[1] - 512
    pair_ref[:, :wide] = both[0, :, :wide]
    pair_ref[:, wide : 2 * wide] = both[1, :, :wide]
    pair_ref[:, 2 * wide : 2 * wide + 512] = both[1, :, rest:]
    if rest > wide:
        total = both[0, :, wide:rest].astype(F32) + both[1, :, wide:rest].astype(F32)
        next_ref[:, : rest - wide] = total.astype(BF)
    next_ref[:, rest - wide :] = both[0, :, rest:]


def step_gram(bit, own, recv):
    level = bit + 1
    wide = (10 - level) * 128
    width = own.shape[1]
    return kcall(
        lambda *r: step_gram_kernel(bit, wide, *r),
        "stepgram",
        [sds((16, 2 * wide + 512)), sds((16, width - wide))],
        [own, recv],
        [pltpu.VMEM((2, 16, width), BF)],
    )


def merge_kernel(p0, p1, p2, p3, out_ref):
    y = ypos_of()
    rows = p0.shape[0]
    for s, p in enumerate((p0, p1, p2, p3)):
        start = pl.multiple_of(((y - s) & 3) * rows, rows)
        out_ref[pl.ds(start, rows), :] = p[...]


def merge(pieces):
    rows, width = pieces[0].shape
    return kcall(merge_kernel, "merge", [sds((4 * rows, width))], pieces)[0]


def unpack_low_kernel(own_ref, recv_ref, w2_ref, w3_ref, k2_ref, k3_ref, both):
    c = core_of()
    both[c] = own_ref[...]
    both[1 - c] = recv_ref[...]
    for cc in range(2):
        for p in range(4):
            rows = both[cc, p * 64 : p * 64 + 64, :]
            w2_ref[p // 2, (p % 2) * 128 + cc * 64 : (p % 2) * 128 + cc * 64 + 64, :] = rows[:, :1024]
            for i in range(2):
                part = rows[:, 1920 + i * 256 : 2176 + i * 256]
                at = cc * 128 + i * 64
                if p in (1, 3):
                    k2_ref[p // 2, at : at + 64, :] = part
                if p == 2:
                    k3_ref[at : at + 64, :] = part
        for h in range(2):
            total = both[cc, h * 128 : h * 128 + 64, 1024:1920].astype(F32) + both[
                cc, h * 128 + 64 : h * 128 + 128, 1024:1920
            ].astype(F32)
            w3_ref[h * 128 + cc * 64 : h * 128 + cc * 64 + 64, :] = total.astype(BF)


def unpack_high_kernel(levels, last, own_ref, recv_ref, *refs):
    outs, both = refs[:-1], refs[-1]
    c = core_of()
    both[c] = own_ref[...]
    both[1 - c] = recv_ref[...]

    def coupling(k_ref, at):
        for cc in range(2):
            for p in range(4):
                rows = both[cc, p * 16 : p * 16 + 16, at : at + 512]
                for i in range(2):
                    to = cc * 128 + i * 64 + p * 16
                    k_ref[to : to + 16, :] = rows[:, i * 256 : i * 256 + 256]

    at = 0
    for n, level in enumerate(levels):
        wide = (10 - level) * 128
        w_ref, k_ref = outs[2 * n], outs[2 * n + 1]
        for half in range(2):
            for cc in range(2):
                to = half * 128 + cc * 64
                w_ref[to : to + 64, :] = both[cc, :, at : at + wide]
            at += wide
        coupling(k_ref, at)
        at += 512
    if last:
        coupling(outs[2 * len(levels)], at)


def unpack_high(levels, last, own, recv):
    outs = []
    for level in levels:
        outs += [sds((256, (10 - level) * 128)), sds((256, 256))]
    if last:
        outs.append(sds((256, 256)))
    return kcall(
        lambda *r: unpack_high_kernel(levels, last, *r),
        "unpackhigh",
        outs,
        [own, recv],
        [pltpu.VMEM((2,) + own.shape, BF)],
    )


def level_one(which, p_ref, own_ref, recv_ref, kown_ref, krecv_ref, w_ref, kboth, pboth):
    c = core_of()
    start = pl.multiple_of((c if which else 1 - c) * HALF, HALF)
    kboth[c] = kown_ref[...]
    kboth[1 - c] = krecv_ref[...]
    pboth[c] = own_ref[pl.ds(start, HALF), :]
    pboth[1 - c] = recv_ref[pl.ds(start, HALF), :]
    rows = kboth[1, pl.ds(pl.multiple_of(c * 128, 128), 128), :]
    factor = (nt(pboth[0], rows[:, :128]) + nt(pboth[1], rows[:, 128:])).astype(BF)
    value = p_ref[pl.ds(start, HALF), :].astype(F32) - nn(factor, w_ref[...])
    return value, factor


def one_send_kernel(p, own, recv, kown, krecv, w, out_ref, f_ref, kboth, pboth):
    value, factor = level_one(0, p, own, recv, kown, krecv, w, kboth, pboth)
    out_ref[...] = value.astype(BF)
    f_ref[...] = factor


def one_keep_kernel(
    p, own, recv, kown, krecv, w, other_ref, o0, o1, o2, o3, f_ref, kboth, pboth, whole
):
    y = ypos_of()
    value, factor = level_one(1, p, own, recv, kown, krecv, w, kboth, pboth)
    f_ref[...] = factor
    whole[...] = value + other_ref[...].astype(F32)
    for s, out in enumerate((o0, o1, o2, o3)):
        start = pl.multiple_of(((y + s) & 3) * NC, 32)
        out[...] = whole[pl.ds(start, NC), :].astype(BF)


def two_three_kernel(
    q0, q1, q2, q3, w2_ref, w3_ref, k2_ref, k3_ref, g_ref, d0, d1, d2, d3, qs, down
):
    y = ypos_of()
    for s, q in enumerate((q0, q1, q2, q3)):
        qs[(y - s) & 3] = q[...]
    sums, factors = [], []
    for h in range(2):
        stacked = jnp.concatenate([qs[2 * h, :, :128], qs[2 * h + 1, :, :128]], axis=1)
        factor = nt(stacked, k2_ref[h]).astype(BF)
        factors.append(factor)
        sums.append(
            qs[2 * h, :, 128:].astype(F32)
            + qs[2 * h + 1, :, 128:].astype(F32)
            - nn(factor, w2_ref[h])
        )
    stacked = jnp.concatenate([sums[0][:, :128], sums[1][:, :128]], axis=1).astype(BF)
    factor = nt(stacked, k3_ref[...]).astype(BF)
    g_ref[...] = (sums[0][:, 128:] + sums[1][:, 128:] - nn(factor, w3_ref[...])).astype(BF)
    for p in range(4):
        h = p // 2
        down[p, :, :128] = factors[h][:, (p % 2) * 128 : (p % 2) * 128 + 128]
        down[p, :, 128:] = factor[:, h * 128 : h * 128 + 128]
    for s, out in enumerate((d0, d1, d2, d3)):
        out[...] = down[(y + s) & 3]


def level_kernel(bit, own_ref, recv_ref, w_ref, k_ref, *refs):
    trend = len(refs) == 5
    if trend:
        kt_ref, f_ref, both, fboth, _ = refs
    else:
        f_ref, g_ref, both, fboth = refs
    side = side_of(bit)
    both[side] = own_ref[:, :128]
    both[1 - side] = recv_ref[:, :128]
    stacked = jnp.concatenate([both[0], both[1]], axis=1)
    factor = nt(stacked, k_ref[...]).astype(BF)
    fboth[0] = factor[:, :128]
    fboth[1] = factor[:, 128:]
    rest = own_ref[:, 128:].astype(F32) + recv_ref[:, 128:].astype(F32) - nn(factor, w_ref[...])
    f_ref[:, :128] = fboth[side]
    if trend:
        f_ref[:, 128:] = nt(rest.astype(BF), kt_ref[...]).astype(BF)
    else:
        g_ref[...] = rest.astype(BF)


def level(bit, own, recv, w, k):
    width = own.shape[1]
    return kcall(
        lambda *r: level_kernel(bit, *r),
        "level",
        [sds((NC, RK)), sds((NC, width - 128))],
        [own, recv, w, k],
        [pltpu.VMEM((2, NC, RK), BF), pltpu.VMEM((2, NC, RK), BF)],
    )


def top(bit, own, recv, w, k, kt):
    return kcall(
        lambda *r: level_kernel(bit, *r),
        "top",
        [sds((NC, 384))],
        [own, recv, w, k, kt],
        [pltpu.VMEM((2, NC, RK), BF), pltpu.VMEM((2, NC, RK), BF), pltpu.VMEM((8, 128), F32)],
    )[0]


def finish_kernel(
    est_ref, v_ref, t_ref, f1s, f1k, fa_own, fa_recv, fb_own, fb_recv, out_ref, factors
):
    @pl.when(pl.program_id(0) == 0)
    def _():
        c = core_of()
        mine = pl.ds(pl.multiple_of(c * HALF, HALF), HALF)
        other = pl.ds(pl.multiple_of((1 - c) * HALF, HALF), HALF)
        factors[other, 0:128] = f1s[...]
        factors[mine, 0:128] = f1k[...]
        factors[mine, 128:384] = fa_own[...]
        factors[other, 128:384] = fa_recv[...]
        factors[mine, 384:1280] = fb_own[...]
        factors[other, 384:1280] = fb_recv[...]

    out_ref[...] = (
        est_ref[...]
        - nt(v_ref[...], factors[:, :1024])
        - nt(t_ref[...], factors[:, 1024:])
    )


def finish(est, v, t, f1s, f1k, fa_own, fa_recv, fb_own, fb_recv):
    rows = 256
    whole = lambda a: pl.BlockSpec(a.shape, lambda j: (0, 0))
    return pl.pallas_call(
        finish_kernel,
        grid=(1024 // rows,),
        in_specs=[
            pl.BlockSpec((rows, 768), lambda j: (j, 0)),
            pl.BlockSpec((rows, 1024), lambda j: (j, 0)),
            pl.BlockSpec((rows, 256), lambda j: (j, 0)),
        ]
        + [whole(a) for a in (f1s, f1k, fa_own, fa_recv, fb_own, fb_recv)],
        out_specs=pl.BlockSpec((rows, 768), lambda j: (j, 0)),
        out_shape=sds((1024, 768), F32),
        scratch_shapes=[pltpu.VMEM((768, 1280), BF)],
        name="finish",
        cost_estimate=pl.CostEstimate(flops=2000000000, bytes_accessed=12000000, transcendentals=0),
    )(est, v, t, f1s, f1k, fa_own, fa_recv, fb_own, fb_recv)


def body(observed, leaf_order, leaf_inverse, project_basis, correct_basis, coupling, trend_basis, trend_correct):
    k_recv = flip(coupling, 0)
    first_gram, g_send, g_keep = kcall(
        gram_kernel,
        "gram",
        [sds((RK, 1152)), sds((64, GW)), sds((64, GW))],
        [project_basis, correct_basis, trend_basis],
        [pltpu.VMEM((RK, GW), F32)],
        flops=1500000000,
    )
    g_recv = flip(g_send, 0)
    est, estt, p1 = leaf_product(leaf_order, observed, leaf_inverse, project_basis)
    p1_recv = flip(p1, 0)

    a, b0, b1, b2, b3 = kcall(
        chip_gram_kernel,
        "chipgram",
        [sds((64, AW))] + [sds((16, BW))] * 4,
        [g_keep, g_recv, coupling, k_recv],
        [pltpu.VMEM((64, BW), F32), pltpu.VMEM((2, 256, 256), BF)],
    )
    a_all = [a] + [turn(a, s) for s in (1, 2, 3)]
    b_all = [b0, turn(b1, 1), turn(b2, 2), turn(b3, 3)]

    pt = project(estt, project_basis, trend_basis)
    boths = [pltpu.VMEM((2, 256, 256), BF), pltpu.VMEM((2, HALF, RK), BF)]
    q_send, f1s = kcall(
        one_send_kernel,
        "onesend",
        [sds((HALF, 1152)), sds((HALF, RK))],
        [pt, p1, p1_recv, coupling, k_recv, first_gram],
        boths,
        flops=400000000,
    )
    q_recv = flip(q_send, 0)
    o0, o1, o2, o3, f1k = kcall(
        one_keep_kernel,
        "onekeep",
        [sds((NC, 1152))] * 4 + [sds((HALF, RK))],
        [pt, p1, p1_recv, coupling, k_recv, first_gram, q_recv],
        boths + [pltpu.VMEM((HALF, 1152), F32)],
        flops=400000000,
    )
    q_all = [o0, turn(o1, 1), turn(o2, 2), turn(o3, 3)]

    a_merged = merge(a_all)
    a_recv = flip(a_merged, 0)
    w2, w3, k2, k3 = kcall(
        unpack_low_kernel,
        "unpacklow",
        [sds((2, 256, 1024)), sds((256, 896)), sds((2, 256, 256)), sds((256, 256))],
        [a_merged, a_recv],
        [pltpu.VMEM((2, 256, AW), BF)],
    )

    state = kcall(
        group_gram_kernel, "groupgram", [sds((16, BW + 512))], b_all + a_all
    )[0]
    pairs = []
    for bit in range(3, 8):
        recv = flip(state, bit)
        pair, state = step_gram(bit, state, recv)
        pairs.append(pair)
    low = jnp.concatenate(pairs[:2], axis=1)
    high = jnp.concatenate(pairs[2:] + [state], axis=1)
    low = merge([low] + [turn(low, s) for s in (1, 2, 3)])
    w4, k4, w5, k5 = unpack_high((4, 5), False, low, flip(low, 0))
    high = merge([high] + [turn(high, s) for s in (1, 2, 3)])
    w6, k6, w7, k7, w8, k8, kt = unpack_high((6, 7, 8), True, high, flip(high, 0))

    g, d0, d1, d2, d3 = kcall(
        two_three_kernel,
        "twothree",
        [sds((NC, 896))] + [sds((NC, 256))] * 4,
        q_all + [w2, w3, k2, k3],
        [pltpu.VMEM((4, NC, 1152), BF), pltpu.VMEM((4, NC, 256), BF)],
    )
    fa = merge([d0, turn(d1, 1), turn(d2, 2), turn(d3, 3)])
    fa_recv = flip(fa, 0)

    factors = []
    for bit, w, k in ((3, w4, k4), (4, w5, k5), (5, w6, k6), (6, w7, k7)):
        f, g = level(bit, g, flip(g, bit), w, k)
        factors.append(f)
    factors.append(top(7, g, flip(g, 7), w8, k8, kt))
    fb = jnp.concatenate(factors, axis=1)
    fb = merge([fb] + [turn(fb, s) for s in (1, 2, 3)])
    fb_recv = flip(fb, 0)
    return finish(est, correct_basis, trend_correct, f1s, f1k, fa, fa_recv, fb, fb_recv)


def solution(mesh):
    placed = P(("outer", "inner"), None)
    return jax.shard_map(
        body, mesh=mesh, in_specs=(placed,) * 8, out_specs=placed, check_vma=False
    )
```
